32 devices in a mesh: theta: 16 (over z, x, core), xr: 2 (over y).
Axes of the slice: x: 2, y: 2, z: 4, core: 2. Of those that a mesh axis runs over, the one named last changes fastest.
Arguments:
- state: float32 [3, 2, 5, 128, 16, 128], P(None, None, None, 'theta', 'xr'), may hold values from -6 to 6
- source: float32 [3, 2, 5, 128, 16, 128], P(None, None, None, 'theta', 'xr'), may hold values from -6 to 6
- sigma: float32 [128, 16, 128], P('theta', 'xr'), may hold values from 0.25 to 4
- stagger: int32 [32], P('theta'), may hold values from 0 to 3
- a_theta: float32 [4, 5, 5], replicated, may hold values from -2.5 to 2.5
- a_axial: float32 [5, 5], replicated, may hold values from -2.5 to 2.5
- a_radial: float32 [5, 5], replicated, may hold values from -2.5 to 2.5
- mode_order: int32 [3, 128], replicated, may hold values from -32 to 32
- mode_radial: int32 [3, 128], replicated, may hold values from 0 to 7
- mode_plane: int32 [3, 128], replicated, may hold values from 0 to 1
- gust: float32 [3, 2, 128], replicated, may hold values from -6 to 6
- l_rows: float32 [2, 5], replicated, may hold values from -4 to 4
- r_cols: float32 [2, 5], replicated, may hold values from -4 to 4
Outputs:
- fields: float32 [3, 2, 5, 128, 16, 128], P(None, None, None, 'theta', 'xr')
- amplitudes: float32 [3, 2, 2, 128], replicated
The draws below stay inside these ranges and needn't reach their ends.
Inputs may be any that keep to these rules, and one draw needn't show every extreme that they name: `mode_plane`: 0 names the inlet plane, 1 the exit plane.
All inputs are finite; a program needn't handle non-finite values.
Results may differ from the reference program's by a relative error of at most 0.0003.
Values sent between devices are 32-bit elements; how exact they have to be, the bound alone decides.
A program may use at most 64 MiB of HBM per device.

```python
import math
import jax
import jax.numpy as jnp
from jax import lax

H = 3
V = 5
STAGGERS = 4
CPP = 4
NR = 128
MODES = 128
M_MAX = 32
NRAD = 8
PASSAGES = 32
NT = 128
NX = 16


def set_ends(array, stream_key, smallest, top_value):
    index_at = [jax.random.randint(jax.random.fold_in(stream_key, axis), (), 0, length) for axis, length in enumerate(array.shape)]
    longest = array.shape.index(max(array.shape))
    neighbour = index_at[:longest] + [(index_at[longest] + 1) % array.shape[longest]] + index_at[longest + 1:]
    return array.at[tuple(index_at)].set(smallest).at[tuple(neighbour)].set(top_value)


def steps_of(stream_key, dims, shards, low, top_value):
    def one(axis_at, blocks):
        steps = jax.random.uniform(jax.random.fold_in(jax.random.fold_in(stream_key, 6), axis_at), (blocks,), jnp.float32, low / len(shards), top_value / len(shards))
        return jnp.repeat(jnp.exp(steps), dims[axis_at] // blocks).reshape((-1,) + (1,) * (len(dims) - axis_at - 1))

    level = one(*shards[0])
    for cut in shards[1:]:
        level = level * one(*cut)
    return level


def bell_draw(key, dims, deviation, reach, split=(), dtype=jnp.bfloat16):
    entries = deviation * jax.random.normal(key, dims, jnp.float32)
    if split:
        entries = entries * steps_of(key, dims, split, -0.22, 0.18)
    return jnp.clip(entries, -reach, reach).astype(dtype)


def setup_inputs(seed: int = 0) -> dict:
    streams_of = jax.random.split(jax.random.key(seed), 14)
    return {
        "state": bell_draw(streams_of[0], (H, 2, V, NT, NX, NR), 1.0, 6.0, ((3, 16), (4, 2)), jnp.float32),
        "source": bell_draw(streams_of[1], (H, 2, V, NT, NX, NR), 1.0, 6.0, ((3, 16), (4, 2)), jnp.float32),
        "sigma": jnp.clip(jnp.exp(math.log(4.0) - 2.7725887 * jax.random.uniform(streams_of[2], (NT, NX, NR), jnp.float32) ** steps_of(streams_of[2], (NT, NX, NR), ((0, 16), (1, 2)), -0.2, 0.2)), 0.25, 4.0),
        "stagger": set_ends(jax.random.randint(streams_of[3], (PASSAGES,), 0, STAGGERS), jax.random.fold_in(streams_of[3], 1), 0, STAGGERS - 1).astype(jnp.int32),
        "a_theta": bell_draw(streams_of[4], (STAGGERS, V, V), V ** -0.5, 2.5, (), jnp.float32),
        "a_axial": bell_draw(streams_of[5], (V, V), V ** -0.5, 2.5, (), jnp.float32),
        "a_radial": bell_draw(streams_of[6], (V, V), V ** -0.5, 2.5, (), jnp.float32),
        "mode_order": set_ends(jax.random.randint(streams_of[7], (H, MODES), 0 - M_MAX, M_MAX + 1), jax.random.fold_in(streams_of[7], 1), 0 - M_MAX, M_MAX).astype(jnp.int32),
        "mode_radial": set_ends(jax.random.randint(streams_of[8], (H, MODES), 0, NRAD), jax.random.fold_in(streams_of[8], 1), 0, NRAD - 1).astype(jnp.int32),
        "mode_plane": set_ends(jax.random.randint(streams_of[9], (H, MODES), 0, 2), jax.random.fold_in(streams_of[9], 1), 0, 1).astype(jnp.int32),
        "gust": bell_draw(streams_of[10], (H, 2, MODES), 1.0, 6.0, (), jnp.float32),
        "l_rows": bell_draw(streams_of[11], (2, V), 1.0, 4.0, (), jnp.float32),
        "r_cols": bell_draw(streams_of[12], (2, V), 1.0, 4.0, (), jnp.float32),
    }


courant = 0.5
viscosity = 0.1
base_frequency = 0.5
highest = lax.Precision.HIGHEST

def reference(state, source, sigma, stagger, a_theta, a_axial, a_radial, mode_order, mode_radial, mode_plane, gust, l_rows, r_cols):
    cells = jnp.arange(NT).astype(jnp.int32)
    cell_matrix = a_theta[stagger[cells // CPP]]
    step_size = courant / (1.0 + sigma)
    scale = 1.0 / math.sqrt(NT * NR)
    radial_pos = jnp.arange(NR).astype(jnp.float32) + 0.5

    def residual(field, freq, forcing):
        diff_theta = (jnp.roll(field, -1, 2) - jnp.roll(field, 1, 2)) * 0.5
        lap_theta = jnp.roll(field, -1, 2) + jnp.roll(field, 1, 2) - 2.0 * field
        padded_x = jnp.pad(field, ((0, 0), (0, 0), (0, 0), (1, 1), (0, 0)))
        diff_axial = (padded_x[:, :, :, 2:] - padded_x[:, :, :, :-2]) * 0.5
        lap_axial = padded_x[:, :, :, 2:] + padded_x[:, :, :, :-2] - 2.0 * field
        padded_r = jnp.pad(field, ((0, 0), (0, 0), (0, 0), (0, 0), (1, 1)))
        diff_radial = (padded_r[..., 2:] - padded_r[..., :-2]) * 0.5
        lap_radial = padded_r[..., 2:] + padded_r[..., :-2] - 2.0 * field
        turned = jnp.stack([-field[1], field[0]])
        flux = jnp.einsum('tvw,pwtxr->pvtxr', cell_matrix, diff_theta, precision=highest)
        flux = flux + jnp.einsum('vw,pwtxr->pvtxr', a_axial, diff_axial, precision=highest)
        flux = flux + jnp.einsum('vw,pwtxr->pvtxr', a_radial, diff_radial, precision=highest)
        return freq * turned + flux - viscosity * (lap_theta + lap_axial + lap_radial) + sigma * field - forcing

    def one_harmonic(items):
        field, forcing, freq, orders, radial, planes, target = items
        first = field - 0.5 * step_size * residual(field, freq, forcing)
        second = field - step_size * residual(first, freq, forcing)
        inlet = jnp.einsum('v,pvtr->ptr', l_rows[0], second[:, :, :, 0, :], precision=highest)
        outlet = jnp.einsum('v,pvtr->ptr', l_rows[1], second[:, :, :, NX - 1, :], precision=highest)
        plane_values = jnp.stack([inlet, outlet])
        angle = 2.0 * math.pi * jnp.mod(orders[:, None] * cells[None, :], NT).astype(jnp.float32) / NT
        cos_table = jnp.cos(angle)
        sin_table = jnp.sin(angle)
        radial_table = jnp.where(radial[:, None] == 0, 1.0, math.sqrt(2.0) * jnp.cos(math.pi * radial[:, None].astype(jnp.float32) * radial_pos[None, :] / NR))
        projected = jnp.einsum('bptr,kr->bptk', plane_values, radial_table, precision=highest)
        amp_real = scale * (jnp.einsum('btk,kt->bk', projected[:, 0], cos_table, precision=highest) + jnp.einsum('btk,kt->bk', projected[:, 1], sin_table, precision=highest))
        amp_imag = scale * (jnp.einsum('btk,kt->bk', projected[:, 1], cos_table, precision=highest) - jnp.einsum('btk,kt->bk', projected[:, 0], sin_table, precision=highest))
        weight = (planes[None, :] == jnp.arange(2)[:, None]).astype(jnp.float32)
        miss_real = weight * (amp_real - target[0][None, :])
        miss_imag = weight * (amp_imag - target[1][None, :])
        coef_real = miss_real[:, :, None] * cos_table[None] - miss_imag[:, :, None] * sin_table[None]
        coef_imag = miss_real[:, :, None] * sin_table[None] + miss_imag[:, :, None] * cos_table[None]
        corr_real = jnp.einsum('bkt,kr->btr', coef_real, radial_table, precision=highest)
        corr_imag = jnp.einsum('bkt,kr->btr', coef_imag, radial_table, precision=highest)
        correction = scale * jnp.stack([corr_real, corr_imag], axis=1)
        second = second.at[:, :, :, 0, :].add(-r_cols[0][None, :, None, None] * correction[0][:, None])
        second = second.at[:, :, :, NX - 1, :].add(-r_cols[1][None, :, None, None] * correction[1][:, None])
        measured = jnp.stack([weight * amp_real, weight * amp_imag], axis=1)
        return (second, measured)
    freqs = base_frequency * (1.0 + jnp.arange(H).astype(jnp.float32))
    fields, amplitudes = lax.map(one_harmonic, (state, source, freqs, mode_order, mode_radial, mode_plane, gust))
    return (fields, amplitudes)
```

```python
import functools
import math

import jax
import jax.numpy as jnp
from jax import lax
from jax.experimental import pallas as pl
from jax.experimental.pallas import tpu as pltpu
from jax.sharding import PartitionSpec as P

courant = 0.5
viscosity = 0.1
base_frequency = 0.5
highest = lax.Precision.HIGHEST
MESH = pl.DeviceIdType.MESH


def kernel(
    dims,
    state_hbm,
    source_hbm,
    sigma_hbm,
    stagger,
    a_theta,
    a_axial,
    a_radial,
    mode_order,
    mode_radial,
    mode_plane,
    gust,
    l_rows,
    r_cols,
    out,
    amps,
    state,
    source,
    sigma,
    first,
    step,
    thalo,
    xhalo,
    xsend,
    phi,
    cosines,
    sines,
    part,
    parts,
    load_sem,
    tsend_sem,
    trecv_sem,
    xsend_sem,
    xrecv_sem,
    psend_sem,
    precv_sem,
):
    T, X, H, V, CT, CX, NR, NPASS, NMODE = dims
    F = 2 * V
    CPP = CT // NPASS
    N = T * X
    th = lax.axis_index("theta")
    xr = lax.axis_index("xr")
    me = th * X + xr
    up = lax.rem(th + 1, T)
    down = lax.rem(th + T - 1, T)
    has_lo = xr > 0
    has_hi = xr < X - 1
    total_theta = CT * T
    scale = 1.0 / math.sqrt(total_theta * NR)

    barrier = pltpu.get_barrier_semaphore()

    @pl.loop(1, N)
    def _(i):
        other = lax.rem(me + i, N)
        pl.semaphore_signal(
            barrier, inc=1, device_id=(other // X, lax.rem(other, X)), device_id_type=MESH
        )

    loads = [
        pltpu.make_async_copy(state_hbm, state.at[:, pl.ds(CX, CT * CX)], load_sem.at[0]),
        pltpu.make_async_copy(sigma_hbm, sigma, load_sem.at[1]),
        pltpu.make_async_copy(source_hbm, source, load_sem.at[2]),
    ]
    for copy in loads:
        copy.start()

    zero = jnp.zeros((H * F, CX, NR), jnp.float32)
    for buf in (state, first):
        buf[:, pl.ds(0, CX)] = zero
        buf[:, pl.ds(CX + CT * CX, CX)] = zero

    def x_rows(row):
        return pl.ds(row, CT, stride=CX)

    loads[0].wait()
    for h in range(H):
        for f in range(F):
            xsend[0, 0, h, f] = state[h * F + f, x_rows(CX + CX - 1), :]
            xsend[0, 1, h, f] = state[h * F + f, x_rows(CX), :]

    pl.semaphore_wait(barrier, N - 1)

    def t_copies(src, offset, stage, h):
        rows = pl.ds(h * F, F)
        return [
            pltpu.make_async_remote_copy(
                src_ref=src.at[rows, pl.ds(offset + (CT - 1) * CX, CX)],
                dst_ref=thalo.at[stage, 0, h],
                send_sem=tsend_sem.at[stage, 0, h],
                recv_sem=trecv_sem.at[stage, 0, h],
                device_id=(up, xr),
                device_id_type=MESH,
            ),
            pltpu.make_async_remote_copy(
                src_ref=src.at[rows, pl.ds(offset, CX)],
                dst_ref=thalo.at[stage, 1, h],
                send_sem=tsend_sem.at[stage, 1, h],
                recv_sem=trecv_sem.at[stage, 1, h],
                device_id=(down, xr),
                device_id_type=MESH,
            ),
        ]

    def x_copy(stage, side, h):
        target = xr + 1 if side == 0 else xr - 1
        return pltpu.make_async_remote_copy(
            src_ref=xsend.at[stage, side, h],
            dst_ref=xhalo.at[stage, side, h],
            send_sem=xsend_sem.at[stage, side, h],
            recv_sem=xrecv_sem.at[stage, side, h],
            device_id=(th, target),
            device_id_type=MESH,
        )

    def send(stage, h):
        for copy in t_copies(state_hbm if stage == 0 else first, 0 if stage == 0 else CX, stage, h):
            copy.start()

        @pl.when(has_hi)
        def _():
            x_copy(stage, 0, h).start()

        @pl.when(has_lo)
        def _():
            x_copy(stage, 1, h).start()

    for h in range(H):
        send(0, h)

    loads[1].wait()
    step[...] = courant / (1.0 + sigma[...])
    loads[2].wait()

    row_id = lax.broadcasted_iota(jnp.int32, (CX, NR), 0)
    lane_id = lax.broadcasted_iota(jnp.int32, (CX, NR), 1)
    first_row = row_id == 0
    last_row = row_id == CX - 1
    first_lane = lane_id == 0
    last_lane = lane_id == NR - 1

    def main(field, result, result_offset, factor):
        @pl.loop(0, H)
        def _(h):
            freq = base_frequency * (h + 1).astype(jnp.float32)

            @pl.loop(0, CT)
            def _(t):
                base = pl.multiple_of(t * CX, CX)
                kind = stagger[t // CPP]
                dt = step[pl.ds(base, CX)]
                if factor != 1.0:
                    dt = factor * dt
                damp = sigma[pl.ds(base, CX)] + 6.0 * viscosity
                at = [[a_theta[kind, v, w] for w in range(V)] for v in range(V)]
                for p in range(2):
                    flux = [None] * V
                    sums = []
                    for w in range(V):
                        f = h * F + p * V + w
                        u = field[f, pl.ds(base + CX, CX)]
                        tm = field[f, pl.ds(base, CX)]
                        tp = field[f, pl.ds(base + 2 * CX, CX)]
                        xm = jnp.where(first_row, 0.0, pltpu.roll(u, 1, 0))
                        xp = jnp.where(last_row, 0.0, pltpu.roll(u, CX - 1, 0))
                        rm = jnp.where(first_lane, 0.0, pltpu.roll(u, 1, 1))
                        rp = jnp.where(last_lane, 0.0, pltpu.roll(u, NR - 1, 1))
                        dth, dx, dr = tp - tm, xp - xm, rp - rm
                        sums.append(((tp + tm) + (xp + xm)) + (rp + rm))
                        for v in range(V):
                            term = (
                                at[v][w] * dth + a_axial[v, w] * dx + a_radial[v, w] * dr
                            )
                            flux[v] = term if flux[v] is None else flux[v] + term
                    for v in range(V):
                        f = h * F + p * V + v
                        u = field[f, pl.ds(base + CX, CX)]
                        other = field[h * F + (1 - p) * V + v, pl.ds(base + CX, CX)]
                        turned = -freq if p == 0 else freq
                        res = (
                            0.5 * flux[v]
                            - viscosity * sums[v]
                            + damp * u
                            + turned * other
                            - source[f, pl.ds(base, CX)]
                        )
                        start = state[f, pl.ds(base + CX, CX)]
                        result[f, pl.ds(base + result_offset, CX)] = start - dt * res

    def halo_terms(values, matrix, sign):
        terms = []
        for v in range(V):
            total = matrix(v, 0) * values[0]
            for w in range(1, V):
                total = total + matrix(v, w) * values[w]
            terms.append((sign * 0.5) * total - viscosity * values[v])
        return terms

    def add_halos(result, offset, stage, h, factor):
        for side, copy in enumerate(t_copies(state_hbm, 0, stage, h)):
            copy.wait_recv()
            t = 0 if side == 0 else CT - 1
            kind = stagger[t // CPP]
            dt = factor * step[pl.ds(t * CX, CX)]
            for p in range(2):
                values = [thalo[stage, side, h, p * V + w] for w in range(V)]
                terms = halo_terms(
                    values, lambda v, w: a_theta[kind, v, w], -1.0 if side == 0 else 1.0
                )
                for v in range(V):
                    at = (h * F + p * V + v, pl.ds(offset + t * CX, CX))
                    result[at] = result[at] - dt * terms[v]
        for side in range(2):

            @pl.when(has_lo if side == 0 else has_hi)
            def _():
                x_copy(stage, side, h).wait_recv()
                x = 0 if side == 0 else CX - 1
                dt = factor * step[x_rows(x), :]
                for p in range(2):
                    values = [xhalo[stage, side, h, p * V + w] for w in range(V)]
                    terms = halo_terms(
                        values, lambda v, w: a_axial[v, w], -1.0 if side == 0 else 1.0
                    )
                    for v in range(V):
                        f = h * F + p * V + v
                        at = (f, x_rows(offset + x), slice(None))
                        result[at] = result[at] - dt * terms[v]

    main(state, first, CX, 0.5)

    cells = (th * CT + lax.broadcasted_iota(jnp.int32, (CT, NMODE), 0)).astype(jnp.float32)
    radial_pos = lax.broadcasted_iota(jnp.int32, (NR, NMODE), 0).astype(jnp.float32) + 0.5
    for h in range(H):
        turns = mode_order[pl.ds(h, 1)].astype(jnp.float32) * cells
        turns = turns - jnp.floor(turns / total_theta) * total_theta
        angle = (2.0 * math.pi) * turns / total_theta
        cosines[h] = jnp.cos(angle)
        sines[h] = jnp.sin(angle)
        radial = mode_radial[pl.ds(h, 1)]
        phi[h] = jnp.where(
            radial == 0,
            1.0,
            math.sqrt(2.0) * jnp.cos(math.pi * radial.astype(jnp.float32) * radial_pos / NR),
        )

    for h in range(H):
        add_halos(first, CX, 0, h, 0.5)
        for f in range(F):
            xsend[1, 0, h, f] = first[h * F + f, x_rows(CX + CX - 1), :]
            xsend[1, 1, h, f] = first[h * F + f, x_rows(CX), :]
        send(1, h)

    main(first, out, 0, 1.0)

    def project(b, h):
        x = 0 if b == 0 else CX - 1
        planes = []
        for p in range(2):
            total = None
            for v in range(V):
                term = l_rows[b, v] * out[h * F + p * V + v, x_rows(x), :]
                total = term if total is None else total + term
            planes.append(total)
        projected = jnp.dot(
            jnp.concatenate(planes, axis=0),
            phi[h],
            precision=highest,
            preferred_element_type=jnp.float32,
        )
        real, imag = projected[:CT], projected[CT:]
        weight = jnp.where(mode_plane[pl.ds(h, 1)] == b, scale, 0.0)
        part_real = jnp.sum(real * cosines[h] + imag * sines[h], axis=0, keepdims=True)
        part_imag = jnp.sum(imag * cosines[h] - real * sines[h], axis=0, keepdims=True)
        part[pl.ds(2 * h, 1)] = weight * part_real
        part[pl.ds(2 * h + 1, 1)] = weight * part_imag

    part[...] = jnp.zeros_like(part)
    for h in range(H):
        add_halos(out, 0, 1, h, 1.0)

        @pl.when(jnp.logical_not(has_lo))
        def _():
            project(0, h)

        @pl.when(jnp.logical_not(has_hi))
        def _():
            project(1, h)

    def part_copy(other):
        return pltpu.make_async_remote_copy(
            src_ref=part,
            dst_ref=parts.at[me],
            send_sem=psend_sem,
            recv_sem=precv_sem,
            device_id=(other // X, lax.rem(other, X)),
            device_id_type=MESH,
        )

    @pl.loop(1, N)
    def _(i):
        part_copy(lax.rem(me + i, N)).start()

    parts[me] = part[...]
    everyone = pltpu.make_async_remote_copy(
        src_ref=parts.at[pl.ds(0, N - 1)],
        dst_ref=parts.at[pl.ds(0, N - 1)],
        send_sem=psend_sem,
        recv_sem=precv_sem,
        device_id=(up, xr),
        device_id_type=MESH,
    )
    everyone.wait_recv()
    total = parts[0]
    if N <= 64:
        for i in range(1, N):
            total = total + parts[i]
    else:
        total = lax.fori_loop(1, N, lambda i, acc: acc + parts[i], total)
    part_rows = [total[i : i + 1] for i in range(2 * H)]
    for h in range(H):
        for b in range(2):
            mine = mode_plane[pl.ds(h, 1)] == b
            for p in range(2):
                amps[h, b, pl.ds(p, 1)] = jnp.where(mine, part_rows[2 * h + p], 0.0)

    def correct(b, h):
        x = 0 if b == 0 else CX - 1
        weight = jnp.where(mode_plane[pl.ds(h, 1)] == b, scale, 0.0)
        real = weight * (part_rows[2 * h] - gust[h, pl.ds(0, 1)])
        imag = weight * (part_rows[2 * h + 1] - gust[h, pl.ds(1, 1)])
        coef = jnp.concatenate(
            [real * cosines[h] - imag * sines[h], real * sines[h] + imag * cosines[h]], axis=0
        )
        q = lax.dot_general(
            coef,
            phi[h],
            (((1,), (1,)), ((), ())),
            precision=highest,
            preferred_element_type=jnp.float32,
        )
        for p in range(2):
            for v in range(V):
                at = (h * F + p * V + v, x_rows(x), slice(None))
                out[at] = out[at] - r_cols[b, v] * q[p * CT : (p + 1) * CT]

    @pl.when(jnp.logical_not(has_lo))
    def _():
        for h in range(H):
            correct(0, h)

    @pl.when(jnp.logical_not(has_hi))
    def _():
        for h in range(H):
            correct(1, h)

    everyone.wait_send()
    for stage in range(2):
        for h in range(H):
            src = state_hbm if stage == 0 else first
            for copy in t_copies(src, 0 if stage == 0 else CX, stage, h):
                copy.wait_send()

            @pl.when(has_hi)
            def _():
                x_copy(stage, 0, h).wait_send()

            @pl.when(has_lo)
            def _():
                x_copy(stage, 1, h).wait_send()


def local(T, X, *args):
    state, source, sigma, stagger = args[:4]
    H, two, V, CT, CX, NR = state.shape
    F = two * V
    NMODE = args[7].shape[1]
    dims = (T, X, H, V, CT, CX, NR, stagger.shape[0], NMODE)
    N = T * X
    rows = CT * CX
    f32 = jnp.float32
    hbm = pl.BlockSpec(memory_space=pl.ANY)
    vmem = pl.BlockSpec(memory_space=pltpu.VMEM)
    smem = pl.BlockSpec(memory_space=pltpu.SMEM)
    DMA = pltpu.SemaphoreType.DMA
    pad = -(-2 * H // 8) * 8
    fields, amplitudes = pl.pallas_call(
        functools.partial(kernel, dims),
        out_shape=(
            jax.ShapeDtypeStruct((H * F, rows, NR), f32),
            jax.ShapeDtypeStruct((H, 2, 2, NMODE), f32),
        ),
        in_specs=[hbm, hbm, hbm, smem, smem, smem, smem, vmem, vmem, vmem, vmem, smem, smem],
        out_specs=(vmem, vmem),
        scratch_shapes=[
            pltpu.VMEM((H * F, rows + 2 * CX, NR), f32),
            pltpu.VMEM((H * F, rows, NR), f32),
            pltpu.VMEM((rows, NR), f32),
            pltpu.VMEM((H * F, rows + 2 * CX, NR), f32),
            pltpu.VMEM((rows, NR), f32),
            pltpu.VMEM((2, 2, H, F, CX, NR), f32),
            pltpu.VMEM((2, 2, H, F, CT, NR), f32),
            pltpu.VMEM((2, 2, H, F, CT, NR), f32),
            pltpu.VMEM((H, NR, NMODE), f32),
            pltpu.VMEM((H, CT, NMODE), f32),
            pltpu.VMEM((H, CT, NMODE), f32),
            pltpu.VMEM((pad, NMODE), f32),
            pltpu.VMEM((N, pad, NMODE), f32),
            DMA((3,)),
            DMA((2, 2, H)),
            DMA((2, 2, H)),
            DMA((2, 2, H)),
            DMA((2, 2, H)),
            DMA,
            DMA,
        ],
        compiler_params=pltpu.CompilerParams(
            collective_id=0, has_side_effects=True, vmem_limit_bytes=40 * 2**20
        ),
        name="wake",
    )(
        state.reshape(H * F, rows, NR),
        source.reshape(H * F, rows, NR),
        sigma.reshape(rows, NR),
        *args[3:],
    )
    return fields.reshape(state.shape), amplitudes


def solution(mesh):
    field = P(None, None, None, "theta", "xr", None)
    placed = (field, field, P("theta", "xr", None), P("theta")) + (P(),) * 9
    return jax.shard_map(
        functools.partial(local, mesh.shape["theta"], mesh.shape["xr"]),
        mesh=mesh,
        in_specs=placed,
        out_specs=(field, P()),
        check_vma=False,
    )
```

```python
import functools
import math

import jax
import jax.numpy as jnp
from jax import lax
from jax.experimental import pallas as pl
from jax.experimental.pallas import tpu as pltpu
from jax.sharding import PartitionSpec as P

courant = 0.5
viscosity = 0.1
base_frequency = 0.5
highest = lax.Precision.HIGHEST
MESH = pl.DeviceIdType.MESH


def kernel(
    dims,
    state_hbm,
    source_hbm,
    sigma_hbm,
    *refs,
):
    small_hbm, refs = refs[:10], refs[10:]
    out, amps, refs = refs[0], refs[1], refs[2:]
    small, refs = refs[:10], refs[10:]
    stagger, a_theta, a_axial, a_radial, l_rows, r_cols = small[:6]
    mode_order, mode_radial, mode_plane, gust = small[6:]
    (
    state,
    source,
    sigma,
    first,
    step,
    thalo,
    xhalo,
    xsend,
    phi,
    cosines,
    sines,
    part,
    parts,
    load_sem,
    tsend_sem,
    trecv_sem,
    xsend_sem,
    xrecv_sem,
    psend_sem,
    precv_sem,
    small_sem,
    ) = refs
    T, X, H, V, CT, CX, NR, NPASS, NMODE = dims
    F = 2 * V
    CPP = CT // NPASS
    N = T * X
    th = lax.axis_index("theta")
    xr = lax.axis_index("xr")
    me = th * X + xr
    up = lax.rem(th + 1, T)
    down = lax.rem(th + T - 1, T)
    has_lo = xr > 0
    has_hi = xr < X - 1
    total_theta = CT * T
    scale = 1.0 / math.sqrt(total_theta * NR)

    barrier = pltpu.get_barrier_semaphore()

    @pl.loop(1, N)
    def _(i):
        other = lax.rem(me + i, N)
        pl.semaphore_signal(
            barrier, inc=1, device_id=(other // X, lax.rem(other, X)), device_id_type=MESH
        )

    little = [
        pltpu.make_async_copy(src, dst, small_sem.at[i])
        for i, (src, dst) in enumerate(zip(small_hbm, small))
    ]
    loads = [
        pltpu.make_async_copy(state_hbm, state.at[:, pl.ds(CX, CT * CX)], load_sem.at[0]),
        pltpu.make_async_copy(sigma_hbm, sigma, load_sem.at[1]),
        pltpu.make_async_copy(source_hbm, source, load_sem.at[2]),
    ]
    for copy in loads + little:
        copy.start()

    zero = jnp.zeros((H * F, CX, NR), jnp.float32)
    for buf in (state, first):
        buf[:, pl.ds(0, CX)] = zero
        buf[:, pl.ds(CX + CT * CX, CX)] = zero

    def x_rows(row):
        return pl.ds(row, CT, stride=CX)

    loads[0].wait()
    for h in range(H):
        for f in range(F):
            xsend[0, 0, h, f] = state[h * F + f, x_rows(CX + CX - 1), :]
            xsend[0, 1, h, f] = state[h * F + f, x_rows(CX), :]

    pl.semaphore_wait(barrier, N - 1)

    def t_copies(src, offset, stage, h):
        rows = pl.ds(h * F, F)
        return [
            pltpu.make_async_remote_copy(
                src_ref=src.at[rows, pl.ds(offset + (CT - 1) * CX, CX)],
                dst_ref=thalo.at[stage, 0, h],
                send_sem=tsend_sem.at[stage, 0, h],
                recv_sem=trecv_sem.at[stage, 0, h],
                device_id=(up, xr),
                device_id_type=MESH,
            ),
            pltpu.make_async_remote_copy(
                src_ref=src.at[rows, pl.ds(offset, CX)],
                dst_ref=thalo.at[stage, 1, h],
                send_sem=tsend_sem.at[stage, 1, h],
                recv_sem=trecv_sem.at[stage, 1, h],
                device_id=(down, xr),
                device_id_type=MESH,
            ),
        ]

    def x_copy(stage, side, h):
        target = xr + 1 if side == 0 else xr - 1
        return pltpu.make_async_remote_copy(
            src_ref=xsend.at[stage, side, h],
            dst_ref=xhalo.at[stage, side, h],
            send_sem=xsend_sem.at[stage, side, h],
            recv_sem=xrecv_sem.at[stage, side, h],
            device_id=(th, target),
            device_id_type=MESH,
        )

    def send(stage, h):
        for copy in t_copies(state_hbm if stage == 0 else first, 0 if stage == 0 else CX, stage, h):
            copy.start()

        @pl.when(has_hi)
        def _():
            x_copy(stage, 0, h).start()

        @pl.when(has_lo)
        def _():
            x_copy(stage, 1, h).start()

    for h in range(H):
        send(0, h)

    for copy in little:
        copy.wait()
    loads[1].wait()
    step[...] = courant / (1.0 + sigma[...])
    loads[2].wait()

    row_id = lax.broadcasted_iota(jnp.int32, (CX, NR), 0)
    lane_id = lax.broadcasted_iota(jnp.int32, (CX, NR), 1)
    first_row = row_id == 0
    last_row = row_id == CX - 1
    first_lane = lane_id == 0
    last_lane = lane_id == NR - 1

    def main(field, result, result_offset, factor):
        @pl.loop(0, H)
        def _(h):
            freq = base_frequency * (h + 1).astype(jnp.float32)

            @pl.loop(0, CT)
            def _(t):
                base = pl.multiple_of(t * CX, CX)
                kind = stagger[t // CPP]
                dt = step[pl.ds(base, CX)]
                if factor != 1.0:
                    dt = factor * dt
                damp = sigma[pl.ds(base, CX)] + 6.0 * viscosity
                at = [[a_theta[v, kind, w] for w in range(V)] for v in range(V)]
                for p in range(2):
                    flux = [None] * V
                    sums = []
                    for w in range(V):
                        f = h * F + p * V + w
                        u = field[f, pl.ds(base + CX, CX)]
                        tm = field[f, pl.ds(base, CX)]
                        tp = field[f, pl.ds(base + 2 * CX, CX)]
                        xm = jnp.where(first_row, 0.0, pltpu.roll(u, 1, 0))
                        xp = jnp.where(last_row, 0.0, pltpu.roll(u, CX - 1, 0))
                        rm = jnp.where(first_lane, 0.0, pltpu.roll(u, 1, 1))
                        rp = jnp.where(last_lane, 0.0, pltpu.roll(u, NR - 1, 1))
                        dth, dx, dr = tp - tm, xp - xm, rp - rm
                        sums.append(((tp + tm) + (xp + xm)) + (rp + rm))
                        for v in range(V):
                            term = (
                                at[v][w] * dth + a_axial[v, w] * dx + a_radial[v, w] * dr
                            )
                            flux[v] = term if flux[v] is None else flux[v] + term
                    for v in range(V):
                        f = h * F + p * V + v
                        u = field[f, pl.ds(base + CX, CX)]
                        other = field[h * F + (1 - p) * V + v, pl.ds(base + CX, CX)]
                        turned = -freq if p == 0 else freq
                        res = (
                            0.5 * flux[v]
                            - viscosity * sums[v]
                            + damp * u
                            + turned * other
                            - source[f, pl.ds(base, CX)]
                        )
                        start = state[f, pl.ds(base + CX, CX)]
                        result[f, pl.ds(base + result_offset, CX)] = start - dt * res

    def halo_terms(values, matrix, sign):
        terms = []
        for v in range(V):
            total = matrix(v, 0) * values[0]
            for w in range(1, V):
                total = total + matrix(v, w) * values[w]
            terms.append((sign * 0.5) * total - viscosity * values[v])
        return terms

    def add_halos(result, offset, stage, h, factor):
        for side, copy in enumerate(t_copies(state_hbm, 0, stage, h)):
            copy.wait_recv()
            t = 0 if side == 0 else CT - 1
            kind = stagger[t // CPP]
            dt = factor * step[pl.ds(t * CX, CX)]
            for p in range(2):
                values = [thalo[stage, side, h, p * V + w] for w in range(V)]
                terms = halo_terms(
                    values, lambda v, w: a_theta[v, kind, w], -1.0 if side == 0 else 1.0
                )
                for v in range(V):
                    at = (h * F + p * V + v, pl.ds(offset + t * CX, CX))
                    result[at] = result[at] - dt * terms[v]
        for side in range(2):

            @pl.when(has_lo if side == 0 else has_hi)
            def _():
                x_copy(stage, side, h).wait_recv()
                x = 0 if side == 0 else CX - 1
                dt = factor * step[x_rows(x), :]
                for p in range(2):
                    values = [xhalo[stage, side, h, p * V + w] for w in range(V)]
                    terms = halo_terms(
                        values, lambda v, w: a_axial[v, w], -1.0 if side == 0 else 1.0
                    )
                    for v in range(V):
                        f = h * F + p * V + v
                        at = (f, x_rows(offset + x), slice(None))
                        result[at] = result[at] - dt * terms[v]

    main(state, first, CX, 0.5)

    cells = (th * CT + lax.broadcasted_iota(jnp.int32, (CT, NMODE), 0)).astype(jnp.float32)
    radial_pos = lax.broadcasted_iota(jnp.int32, (NR, NMODE), 0).astype(jnp.float32) + 0.5
    for h in range(H):
        turns = mode_order[pl.ds(h, 1)].astype(jnp.float32) * cells
        turns = turns - jnp.floor(turns / total_theta) * total_theta
        angle = (2.0 * math.pi) * turns / total_theta
        cosines[h] = jnp.cos(angle)
        sines[h] = jnp.sin(angle)
        radial = mode_radial[pl.ds(h, 1)]
        phi[h] = jnp.where(
            radial == 0,
            1.0,
            math.sqrt(2.0) * jnp.cos(math.pi * radial.astype(jnp.float32) * radial_pos / NR),
        )

    for h in range(H):
        add_halos(first, CX, 0, h, 0.5)
        for f in range(F):
            xsend[1, 0, h, f] = first[h * F + f, x_rows(CX + CX - 1), :]
            xsend[1, 1, h, f] = first[h * F + f, x_rows(CX), :]
        send(1, h)

    main(first, out, 0, 1.0)

    def project(b, h):
        x = 0 if b == 0 else CX - 1
        planes = []
        for p in range(2):
            total = None
            for v in range(V):
                term = l_rows[b, v] * out[h * F + p * V + v, x_rows(x), :]
                total = term if total is None else total + term
            planes.append(total)
        projected = jnp.dot(
            jnp.concatenate(planes, axis=0),
            phi[h],
            precision=highest,
            preferred_element_type=jnp.float32,
        )
        real, imag = projected[:CT], projected[CT:]
        weight = jnp.where(mode_plane[pl.ds(h, 1)] == b, scale, 0.0)
        part_real = jnp.sum(real * cosines[h] + imag * sines[h], axis=0, keepdims=True)
        part_imag = jnp.sum(imag * cosines[h] - real * sines[h], axis=0, keepdims=True)
        part[pl.ds(2 * h, 1)] = weight * part_real
        part[pl.ds(2 * h + 1, 1)] = weight * part_imag

    part[...] = jnp.zeros_like(part)
    for h in range(H):
        add_halos(out, 0, 1, h, 1.0)

        @pl.when(jnp.logical_not(has_lo))
        def _():
            project(0, h)

        @pl.when(jnp.logical_not(has_hi))
        def _():
            project(1, h)

    def part_copy(other):
        return pltpu.make_async_remote_copy(
            src_ref=part,
            dst_ref=parts.at[me],
            send_sem=psend_sem,
            recv_sem=precv_sem,
            device_id=(other // X, lax.rem(other, X)),
            device_id_type=MESH,
        )

    @pl.loop(1, N)
    def _(i):
        part_copy(lax.rem(me + i, N)).start()

    parts[me] = part[...]
    everyone = pltpu.make_async_remote_copy(
        src_ref=parts.at[pl.ds(0, N - 1)],
        dst_ref=parts.at[pl.ds(0, N - 1)],
        send_sem=psend_sem,
        recv_sem=precv_sem,
        device_id=(up, xr),
        device_id_type=MESH,
    )
    everyone.wait_recv()
    total = parts[0]
    if N <= 64:
        for i in range(1, N):
            total = total + parts[i]
    else:
        total = lax.fori_loop(1, N, lambda i, acc: acc + parts[i], total)
    part_rows = [total[i : i + 1] for i in range(2 * H)]
    for h in range(H):
        for b in range(2):
            mine = mode_plane[pl.ds(h, 1)] == b
            for p in range(2):
                amps[h, b, pl.ds(p, 1)] = jnp.where(mine, part_rows[2 * h + p], 0.0)

    def correct(b, h):
        x = 0 if b == 0 else CX - 1
        weight = jnp.where(mode_plane[pl.ds(h, 1)] == b, scale, 0.0)
        real = weight * (part_rows[2 * h] - gust[h, pl.ds(0, 1)])
        imag = weight * (part_rows[2 * h + 1] - gust[h, pl.ds(1, 1)])
        coef = jnp.concatenate(
            [real * cosines[h] - imag * sines[h], real * sines[h] + imag * cosines[h]], axis=0
        )
        q = lax.dot_general(
            coef,
            phi[h],
            (((1,), (1,)), ((), ())),
            precision=highest,
            preferred_element_type=jnp.float32,
        )
        for p in range(2):
            for v in range(V):
                at = (h * F + p * V + v, x_rows(x), slice(None))
                out[at] = out[at] - r_cols[b, v] * q[p * CT : (p + 1) * CT]

    @pl.when(jnp.logical_not(has_lo))
    def _():
        for h in range(H):
            correct(0, h)

    @pl.when(jnp.logical_not(has_hi))
    def _():
        for h in range(H):
            correct(1, h)

    everyone.wait_send()
    for stage in range(2):
        for h in range(H):
            src = state_hbm if stage == 0 else first
            for copy in t_copies(src, 0 if stage == 0 else CX, stage, h):
                copy.wait_send()

            @pl.when(has_hi)
            def _():
                x_copy(stage, 0, h).wait_send()

            @pl.when(has_lo)
            def _():
                x_copy(stage, 1, h).wait_send()


def store_kernel(fields, amps, fields_out, amps_out, sems):
    copies = [
        pltpu.make_async_copy(fields, fields_out, sems.at[0]),
        pltpu.make_async_copy(amps, amps_out, sems.at[1]),
    ]
    for copy in copies:
        copy.start()
    for copy in copies:
        copy.wait()


def store(fields, amps):
    vmem = pl.BlockSpec(memory_space=pl.ANY)
    hbm = pl.BlockSpec(memory_space=pltpu.HBM)
    return pl.pallas_call(
        store_kernel,
        out_shape=tuple(jax.ShapeDtypeStruct(a.shape, a.dtype) for a in (fields, amps)),
        in_specs=(vmem, vmem),
        out_specs=(hbm, hbm),
        compiler_params=pltpu.CompilerParams(vmem_limit_bytes=2**20),
        scratch_shapes=[pltpu.SemaphoreType.DMA((2,))],
        name="store",
    )(fields, amps)


def local(T, X, *args):
    state, source, sigma, stagger = args[:4]
    H, two, V, CT, CX, NR = state.shape
    F = two * V
    NMODE = args[7].shape[1]
    dims = (T, X, H, V, CT, CX, NR, stagger.shape[0], NMODE)
    N = T * X
    rows = CT * CX
    f32 = jnp.float32
    hbm = pl.BlockSpec(memory_space=pl.ANY)
    vmem = pl.BlockSpec(memory_space=pltpu.VMEM)
    DMA = pltpu.SemaphoreType.DMA
    stagger, a_theta, a_axial, a_radial, orders, radial, planes, gust, l_rows, r_cols = args[3:]
    small = [stagger, jnp.swapaxes(a_theta, 0, 1), a_axial, a_radial, l_rows, r_cols]
    small += [orders, radial, planes, gust]
    pad = -(-2 * H // 8) * 8
    fields, amplitudes = pl.pallas_call(
        functools.partial(kernel, dims),
        out_shape=(
            jax.ShapeDtypeStruct((H * F, rows, NR), f32),
            jax.ShapeDtypeStruct((H, 2, 2, NMODE), f32),
        ),
        in_specs=[hbm] * 13,
        out_specs=(vmem, vmem),
        scratch_shapes=[pltpu.SMEM(a.shape, a.dtype) for a in small[:6]]
        + [pltpu.VMEM(a.shape, a.dtype) for a in small[6:]]
        + [
            pltpu.VMEM((H * F, rows + 2 * CX, NR), f32),
            pltpu.VMEM((H * F, rows, NR), f32),
            pltpu.VMEM((rows, NR), f32),
            pltpu.VMEM((H * F, rows + 2 * CX, NR), f32),
            pltpu.VMEM((rows, NR), f32),
            pltpu.VMEM((2, 2, H, F, CX, NR), f32),
            pltpu.VMEM((2, 2, H, F, CT, NR), f32),
            pltpu.VMEM((2, 2, H, F, CT, NR), f32),
            pltpu.VMEM((H, NR, NMODE), f32),
            pltpu.VMEM((H, CT, NMODE), f32),
            pltpu.VMEM((H, CT, NMODE), f32),
            pltpu.VMEM((pad, NMODE), f32),
            pltpu.VMEM((N, pad, NMODE), f32),
            DMA((3,)),
            DMA((2, 2, H)),
            DMA((2, 2, H)),
            DMA((2, 2, H)),
            DMA((2, 2, H)),
            DMA,
            DMA,
            DMA((10,)),
        ],
        compiler_params=pltpu.CompilerParams(
            collective_id=0, has_side_effects=True, vmem_limit_bytes=16 * 2**20
        ),
        name="wake",
    )(
        *(pltpu.with_memory_space_constraint(a, pltpu.HBM) for a in (state.reshape(H * F, rows, NR),
        source.reshape(H * F, rows, NR),
        sigma.reshape(rows, NR),
        *small)),
    )
    fields, amplitudes = store(fields, amplitudes)
    return fields.reshape(state.shape), amplitudes


def solution(mesh):
    field = P(None, None, None, "theta", "xr", None)
    placed = (field, field, P("theta", "xr", None), P("theta")) + (P(),) * 9
    return jax.shard_map(
        functools.partial(local, mesh.shape["theta"], mesh.shape["xr"]),
        mesh=mesh,
        in_specs=placed,
        out_specs=(field, P()),
        check_vma=False,
    )
```

```python
import functools
import math

import jax
import jax.numpy as jnp
from jax import lax
from jax.experimental import pallas as pl
from jax.experimental.pallas import tpu as pltpu
from jax.sharding import PartitionSpec as P

courant = 0.5
viscosity = 0.1
base_frequency = 0.5
highest = lax.Precision.HIGHEST
MESH = pl.DeviceIdType.MESH


def kernel(
    dims,
    state_hbm,
    source_hbm,
    sigma_hbm,
    *refs,
):
    small_hbm, refs = refs[:10], refs[10:]
    out, amps, refs = refs[0], refs[1], refs[2:]
    small, refs = refs[:10], refs[10:]
    stagger, a_theta, a_axial, a_radial, l_rows, r_cols = small[:6]
    mode_order, mode_radial, mode_plane, gust = small[6:]
    (
    state,
    source,
    sigma,
    first,
    step,
    thalo,
    xhalo,
    xsend,
    phi,
    phi_t,
    cosines,
    sines,
    part,
    parts,
    load_sem,
    tsend_sem,
    trecv_sem,
    xsend_sem,
    xrecv_sem,
    psend_sem,
    precv_sem,
    small_sem,
    kinds,
    ghost_sigma,
    ghost_kind,
    weights,
    isend_sem,
    irecv_sem,
    ) = refs
    T, X, H, V, CT, CX, NR, NPASS, NMODE = dims
    F = 2 * V
    CPP = CT // NPASS
    N = T * X
    th = lax.axis_index("theta")
    xr = lax.axis_index("xr")
    me = th * X + xr
    up = lax.rem(th + 1, T)
    down = lax.rem(th + T - 1, T)
    has_lo = xr > 0
    has_hi = xr < X - 1
    total_theta = CT * T
    scale = 1.0 / math.sqrt(total_theta * NR)

    barrier = pltpu.get_barrier_semaphore()

    def for_others(act):
        for x in range(X):

            @pl.when(x != xr)
            def _():
                act(th, x)

        def ring(j):
            far = th + j
            far = jnp.where(far >= T, far - T, far)
            for x in range(X):
                act(far, x)

        if T * X <= 64:
            for j in range(1, T):
                ring(j)
        else:
            pl.loop(1, T)(ring)

    def greet(t, x):
        pl.semaphore_signal(barrier, inc=1, device_id=(t, x), device_id_type=MESH)

    for_others(greet)

    little = [
        pltpu.make_async_copy(src, dst, small_sem.at[i])
        for i, (src, dst) in enumerate(zip(small_hbm, small))
    ]
    loads = [
        pltpu.make_async_copy(state_hbm, state.at[:, pl.ds(CX, CT * CX)], load_sem.at[0]),
        pltpu.make_async_copy(sigma_hbm, sigma, load_sem.at[1]),
        pltpu.make_async_copy(source_hbm, source, load_sem.at[2]),
    ]
    for copy in loads + little:
        copy.start()

    zero = jnp.zeros((H * F, CX, NR), jnp.float32)
    for buf in (state, first):
        buf[:, pl.ds(0, CX)] = zero
        buf[:, pl.ds(CX + CT * CX, CX)] = zero

    def x_rows(row):
        return pl.ds(row, CT, stride=CX)

    pl.semaphore_wait(barrier, N - 1)

    def t_copies(src, offset, stage, h):
        rows = pl.ds(h * F, F)
        return [
            pltpu.make_async_remote_copy(
                src_ref=src.at[rows, pl.ds(offset + (CT - 1) * CX, CX)],
                dst_ref=thalo.at[stage, 0, h],
                send_sem=tsend_sem.at[stage, 0, h],
                recv_sem=trecv_sem.at[stage, 0, h],
                device_id=(up, xr),
                device_id_type=MESH,
            ),
            pltpu.make_async_remote_copy(
                src_ref=src.at[rows, pl.ds(offset, CX)],
                dst_ref=thalo.at[stage, 1, h],
                send_sem=tsend_sem.at[stage, 1, h],
                recv_sem=trecv_sem.at[stage, 1, h],
                device_id=(down, xr),
                device_id_type=MESH,
            ),
        ]

    def x_copy(stage, side, h):
        target = xr + 1 if side == 0 else xr - 1
        return pltpu.make_async_remote_copy(
            src_ref=xsend.at[stage, side, h],
            dst_ref=xhalo.at[stage, side, h],
            send_sem=xsend_sem.at[stage, side, h],
            recv_sem=xrecv_sem.at[stage, side, h],
            device_id=(th, target),
            device_id_type=MESH,
        )

    def send_t(stage, h):
        for copy in t_copies(state_hbm if stage == 0 else first, 0 if stage == 0 else CX, stage, h):
            copy.start()

    def send_x(field, stage, h):
        for f in range(F):
            xsend[stage, 0, h, f] = field[h * F + f, x_rows(CX + CX - 1), :]
            xsend[stage, 1, h, f] = field[h * F + f, x_rows(CX), :]

        @pl.when(has_hi)
        def _():
            x_copy(stage, 0, h).start()

        @pl.when(has_lo)
        def _():
            x_copy(stage, 1, h).start()

    def info_copy(what, side):
        src = sigma_hbm.at[pl.ds((CT - 1) * CX if side == 0 else 0, CX)]
        return pltpu.make_async_remote_copy(
            src_ref=src if what == 0 else kinds.at[side],
            dst_ref=(ghost_sigma if what == 0 else ghost_kind).at[side],
            send_sem=isend_sem.at[what, side],
            recv_sem=irecv_sem.at[what, side],
            device_id=(up if side == 0 else down, xr),
            device_id_type=MESH,
        )

    for side in range(2):
        info_copy(0, side).start()
    for h in range(H):
        send_t(0, h)
    for copy in little:
        copy.wait()
    for side in range(2):
        kind = stagger[NPASS - 1 if side == 0 else 0].astype(jnp.float32)
        kinds[side] = jnp.full((8, NR), kind, jnp.float32)
        info_copy(1, side).start()
    loads[0].wait()
    for h in range(H):
        send_x(state, 0, h)

    loads[1].wait()
    step[...] = courant / (1.0 + sigma[...])
    loads[2].wait()

    row_id = lax.broadcasted_iota(jnp.int32, (CX, NR), 0)
    lane_id = lax.broadcasted_iota(jnp.int32, (CX, NR), 1)
    first_row = row_id == 0
    last_row = row_id == CX - 1
    first_lane = lane_id == 0
    last_lane = lane_id == NR - 1

    def main(field, result, result_offset, factor):
        @pl.loop(0, H)
        def _(h):
            freq = base_frequency * (h + 1).astype(jnp.float32)

            @pl.loop(0, CT)
            def _(t):
                base = pl.multiple_of(t * CX, CX)
                kind = stagger[t // CPP]
                dt = step[pl.ds(base, CX)]
                if factor != 1.0:
                    dt = factor * dt
                damp = sigma[pl.ds(base, CX)] + 6.0 * viscosity
                at = [[a_theta[v, kind, w] for w in range(V)] for v in range(V)]
                for p in range(2):
                    flux = [None] * V
                    sums = []
                    for w in range(V):
                        f = h * F + p * V + w
                        u = field[f, pl.ds(base + CX, CX)]
                        tm = field[f, pl.ds(base, CX)]
                        tp = field[f, pl.ds(base + 2 * CX, CX)]
                        xm = jnp.where(first_row, 0.0, pltpu.roll(u, 1, 0))
                        xp = jnp.where(last_row, 0.0, pltpu.roll(u, CX - 1, 0))
                        rm = jnp.where(first_lane, 0.0, pltpu.roll(u, 1, 1))
                        rp = jnp.where(last_lane, 0.0, pltpu.roll(u, NR - 1, 1))
                        dth, dx, dr = tp - tm, xp - xm, rp - rm
                        sums.append(((tp + tm) + (xp + xm)) + (rp + rm))
                        for v in range(V):
                            term = (
                                at[v][w] * dth + a_axial[v, w] * dx + a_radial[v, w] * dr
                            )
                            flux[v] = term if flux[v] is None else flux[v] + term
                    for v in range(V):
                        f = h * F + p * V + v
                        u = field[f, pl.ds(base + CX, CX)]
                        other = field[h * F + (1 - p) * V + v, pl.ds(base + CX, CX)]
                        turned = -freq if p == 0 else freq
                        res = (
                            0.5 * flux[v]
                            - viscosity * sums[v]
                            + damp * u
                            + turned * other
                            - source[f, pl.ds(base, CX)]
                        )
                        start = state[f, pl.ds(base + CX, CX)]
                        result[f, pl.ds(base + result_offset, CX)] = start - dt * res

    def halo_terms(values, matrix, sign):
        terms = []
        for v in range(V):
            total = matrix(v, 0) * values[0]
            for w in range(1, V):
                total = total + matrix(v, w) * values[w]
            terms.append((sign * 0.5) * total - viscosity * values[v])
        return terms

    def add_t_halos(result, offset, stage, h, factor):
        for side, copy in enumerate(t_copies(state_hbm, 0, stage, h)):
            copy.wait_recv()
            t = 0 if side == 0 else CT - 1
            kind = stagger[t // CPP]
            dt = factor * step[pl.ds(t * CX, CX)]
            for p in range(2):
                values = [thalo[stage, side, h, p * V + w] for w in range(V)]
                terms = halo_terms(
                    values, lambda v, w: a_theta[v, kind, w], -1.0 if side == 0 else 1.0
                )
                for v in range(V):
                    at = (h * F + p * V + v, pl.ds(offset + t * CX, CX))
                    result[at] = result[at] - dt * terms[v]

    def add_x_halos(result, offset, stage, h, factor):
        for side in range(2):

            @pl.when(has_lo if side == 0 else has_hi)
            def _():
                x_copy(stage, side, h).wait_recv()
                x = 0 if side == 0 else CX - 1
                dt = factor * step[x_rows(x), :]
                for p in range(2):
                    values = [xhalo[stage, side, h, p * V + w] for w in range(V)]
                    terms = halo_terms(
                        values, lambda v, w: a_axial[v, w], -1.0 if side == 0 else 1.0
                    )
                    for v in range(V):
                        f = h * F + p * V + v
                        at = (f, x_rows(offset + x), slice(None))
                        result[at] = result[at] - dt * terms[v]

    main(state, first, CX, 0.5)

    cells = lax.broadcasted_iota(jnp.int32, (2 * CT, NMODE), 0)
    cells = (th * CT + jnp.where(cells == CT + 1, -1, cells)).astype(jnp.float32)
    radial_pos = lax.broadcasted_iota(jnp.int32, (NR, NMODE), 0).astype(jnp.float32) + 0.5
    for h in range(H):
        turns = mode_order[pl.ds(h, 1)].astype(jnp.float32) * cells
        turns = turns - jnp.floor(turns / total_theta) * total_theta
        angle = (2.0 * math.pi) * turns / total_theta
        cosines[h] = jnp.cos(angle)
        sines[h] = jnp.sin(angle)
        radial = mode_radial[pl.ds(h, 1)]
        table = jnp.where(
            radial == 0,
            1.0,
            math.sqrt(2.0) * jnp.cos(math.pi * radial.astype(jnp.float32) * radial_pos / NR),
        )
        phi[h] = table
        phi_t[h] = table.T

    for what in range(2):
        for side in range(2):
            info_copy(what, side).wait_recv()

    def edge_weights(b):
        x = 0 if b == 0 else CX - 1
        for side in range(2):
            dt = courant / (1.0 + ghost_sigma[side, pl.ds(x, 1)])
            kind = ghost_kind[side, pl.ds(0, 1)]
            masks = [kind == float(k) for k in range(a_theta.shape[1])]
            for w in range(V):
                total = jnp.zeros((1, NR), jnp.float32)
                for k, mask in enumerate(masks):
                    row = l_rows[b, 0] * a_theta[0, k, w]
                    for v in range(1, V):
                        row = row + l_rows[b, v] * a_theta[v, k, w]
                    total = jnp.where(mask, row, total)
                total = (0.5 if side == 0 else -0.5) * total - viscosity * l_rows[b, w]
                weights[b, side, pl.ds(w, 1)] = -dt * total

    @pl.when(jnp.logical_not(has_lo))
    def _():
        edge_weights(0)

    @pl.when(jnp.logical_not(has_hi))
    def _():
        edge_weights(1)

    for h in range(H):
        add_x_halos(first, CX, 0, h, 0.5)
        add_t_halos(first, CX, 0, h, 0.5)
        send_t(1, h)
        send_x(first, 1, h)

    def plane_value(b, h, p):
        x = 0 if b == 0 else CX - 1
        inner = 1 if b == 0 else CX - 2
        lines = lax.broadcasted_iota(jnp.int32, (CT, NR), 0)
        freq = base_frequency * (h + 1.0)
        flux = start = sums = fields = others = forcing = 0.0
        for w in range(V):
            f = h * F + p * V + w
            l = l_rows[b, w]
            u = first[f, x_rows(CX + x), :]
            near = first[f, x_rows(CX + inner), :]
            tm = jnp.where(lines == 0, 0.0, pltpu.roll(u, 1, 0))
            tp = jnp.where(lines == CT - 1, 0.0, pltpu.roll(u, CT - 1, 0))
            rm = jnp.where(first_lane, 0.0, pltpu.roll(u, 1, 1))
            rp = jnp.where(last_lane, 0.0, pltpu.roll(u, NR - 1, 1))
            gx = gr = 0.0
            for v in range(V):
                gx = gx + l_rows[b, v] * a_axial[v, w]
                gr = gr + l_rows[b, v] * a_radial[v, w]
            gt = None
            for k in range(NPASS):
                row = 0.0
                for v in range(V):
                    row = row + l_rows[b, v] * a_theta[v, stagger[k], w]
                gt = row if gt is None else jnp.where(lines >= k * CPP, row, gt)
            dx = near if b == 0 else -near
            flux = flux + (gt * (tp - tm) + gx * dx + gr * (rp - rm))
            sums = sums + l * ((tp + tm) + near + (rp + rm))
            fields = fields + l * u
            others = others + l * first[h * F + (1 - p) * V + w, x_rows(CX + x), :]
            forcing = forcing + l * source[f, x_rows(x), :]
            start = start + l * state[f, x_rows(CX + x), :]
        damp = sigma[x_rows(x), :] + 6.0 * viscosity
        turned = -freq if p == 0 else freq
        res = 0.5 * flux - viscosity * sums + damp * fields + turned * others - forcing
        return start - step[x_rows(x), :] * res

    def project(b, h):
        x = 0 if b == 0 else CX - 1
        planes = []
        for p in range(2):
            planes.append(plane_value(b, h, p))
            edges = []
            for side in range(2):
                row = CX + x + (0 if side == 0 else (CT - 1) * CX)
                edge = None
                for w in range(V):
                    term = weights[b, side, pl.ds(w, 1)] * first[h * F + p * V + w, pl.ds(row, 1)]
                    edge = term if edge is None else edge + term
                edges.append(edge)
            lines = lax.broadcasted_iota(jnp.int32, (CT, NR), 0)
            planes.append(
                jnp.where(lines == 0, edges[1], jnp.where(lines == 1, edges[0], 0.0))
            )
        projected = jnp.dot(
            jnp.concatenate(planes, axis=0),
            phi[h],
            precision=highest,
            preferred_element_type=jnp.float32,
        )
        real, imag = projected[: 2 * CT], projected[2 * CT :]
        weight = jnp.where(mode_plane[pl.ds(h, 1)] == b, scale, 0.0)
        part_real = jnp.sum(real * cosines[h] + imag * sines[h], axis=0, keepdims=True)
        part_imag = jnp.sum(imag * cosines[h] - real * sines[h], axis=0, keepdims=True)
        part[pl.ds(2 * h, 1)] = weight * part_real
        part[pl.ds(2 * h + 1, 1)] = weight * part_imag

    part[...] = jnp.zeros_like(part)
    for h in range(H):

        @pl.when(jnp.logical_not(has_lo))
        def _():
            project(0, h)

        @pl.when(jnp.logical_not(has_hi))
        def _():
            project(1, h)

    def share(t, x):
        copy = pltpu.make_async_remote_copy(
            src_ref=part,
            dst_ref=parts.at[me],
            send_sem=psend_sem,
            recv_sem=precv_sem,
            device_id=(t, x),
            device_id_type=MESH,
        )
        copy.start()

    for_others(share)
    parts[me] = part[...]
    main(first, out, 0, 1.0)
    for h in range(H):
        add_t_halos(out, 0, 1, h, 1.0)
        add_x_halos(out, 0, 1, h, 1.0)
    everyone = pltpu.make_async_remote_copy(
        src_ref=parts.at[pl.ds(0, N - 1)],
        dst_ref=parts.at[pl.ds(0, N - 1)],
        send_sem=psend_sem,
        recv_sem=precv_sem,
        device_id=(up, xr),
        device_id_type=MESH,
    )
    everyone.wait_recv()
    total = parts[0]
    if N <= 64:
        for i in range(1, N):
            total = total + parts[i]
    else:
        total = lax.fori_loop(1, N, lambda i, acc: acc + parts[i], total)
    part_rows = [total[i : i + 1] for i in range(2 * H)]
    for h in range(H):
        for b in range(2):
            mine = mode_plane[pl.ds(h, 1)] == b
            for p in range(2):
                amps[h, b, pl.ds(p, 1)] = jnp.where(mine, part_rows[2 * h + p], 0.0)

    def correct(b, h):
        x = 0 if b == 0 else CX - 1
        weight = jnp.where(mode_plane[pl.ds(h, 1)] == b, scale, 0.0)
        real = weight * (part_rows[2 * h] - gust[h, pl.ds(0, 1)])
        imag = weight * (part_rows[2 * h + 1] - gust[h, pl.ds(1, 1)])
        cos, sin = cosines[h, pl.ds(0, CT)], sines[h, pl.ds(0, CT)]
        coef = jnp.concatenate(
            [real * cos - imag * sin, real * sin + imag * cos], axis=0
        )
        q = jnp.dot(
            coef,
            phi_t[h],
            precision=highest,
            preferred_element_type=jnp.float32,
        )
        for p in range(2):
            for v in range(V):
                at = (h * F + p * V + v, x_rows(x), slice(None))
                out[at] = out[at] - r_cols[b, v] * q[p * CT : (p + 1) * CT]

    @pl.when(jnp.logical_not(has_lo))
    def _():
        for h in range(H):
            correct(0, h)

    @pl.when(jnp.logical_not(has_hi))
    def _():
        for h in range(H):
            correct(1, h)

    everyone.wait_send()
    for what in range(2):
        for side in range(2):
            info_copy(what, side).wait_send()
    for stage in range(2):
        for h in range(H):
            src = state_hbm if stage == 0 else first
            for copy in t_copies(src, 0 if stage == 0 else CX, stage, h):
                copy.wait_send()

            @pl.when(has_hi)
            def _():
                x_copy(stage, 0, h).wait_send()

            @pl.when(has_lo)
            def _():
                x_copy(stage, 1, h).wait_send()


def store_kernel(fields, amps, fields_out, amps_out, sems):
    copies = [
        pltpu.make_async_copy(fields, fields_out, sems.at[0]),
        pltpu.make_async_copy(amps, amps_out, sems.at[1]),
    ]
    for copy in copies:
        copy.start()
    for copy in copies:
        copy.wait()


def store(fields, amps):
    vmem = pl.BlockSpec(memory_space=pl.ANY)
    hbm = pl.BlockSpec(memory_space=pltpu.HBM)
    return pl.pallas_call(
        store_kernel,
        out_shape=tuple(jax.ShapeDtypeStruct(a.shape, a.dtype) for a in (fields, amps)),
        in_specs=(vmem, vmem),
        out_specs=(hbm, hbm),
        compiler_params=pltpu.CompilerParams(vmem_limit_bytes=2**20),
        scratch_shapes=[pltpu.SemaphoreType.DMA((2,))],
        name="store",
    )(fields, amps)


def local(T, X, *args):
    state, source, sigma, stagger = args[:4]
    H, two, V, CT, CX, NR = state.shape
    F = two * V
    NMODE = args[7].shape[1]
    dims = (T, X, H, V, CT, CX, NR, stagger.shape[0], NMODE)
    N = T * X
    rows = CT * CX
    f32 = jnp.float32
    hbm = pl.BlockSpec(memory_space=pl.ANY)
    vmem = pl.BlockSpec(memory_space=pltpu.VMEM)
    DMA = pltpu.SemaphoreType.DMA
    stagger, a_theta, a_axial, a_radial, orders, radial, planes, gust, l_rows, r_cols = args[3:]
    small = [stagger, jnp.swapaxes(a_theta, 0, 1), a_axial, a_radial, l_rows, r_cols]
    small += [orders, radial, planes, gust]
    pad = -(-2 * H // 8) * 8
    fields, amplitudes = pl.pallas_call(
        functools.partial(kernel, dims),
        out_shape=(
            jax.ShapeDtypeStruct((H * F, rows, NR), f32),
            jax.ShapeDtypeStruct((H, 2, 2, NMODE), f32),
        ),
        in_specs=[hbm] * 13,
        out_specs=(vmem, vmem),
        scratch_shapes=[pltpu.SMEM(a.shape, a.dtype) for a in small[:6]]
        + [pltpu.VMEM(a.shape, a.dtype) for a in small[6:]]
        + [
            pltpu.VMEM((H * F, rows + 2 * CX, NR), f32),
            pltpu.VMEM((H * F, rows, NR), f32),
            pltpu.VMEM((rows, NR), f32),
            pltpu.VMEM((H * F, rows + 2 * CX, NR), f32),
            pltpu.VMEM((rows, NR), f32),
            pltpu.VMEM((2, 2, H, F, CX, NR), f32),
            pltpu.VMEM((2, 2, H, F, CT, NR), f32),
            pltpu.VMEM((2, 2, H, F, CT, NR), f32),
            pltpu.VMEM((H, NR, NMODE), f32),
            pltpu.VMEM((H, NMODE, NR), f32),
            pltpu.VMEM((H, 2 * CT, NMODE), f32),
            pltpu.VMEM((H, 2 * CT, NMODE), f32),
            pltpu.VMEM((pad, NMODE), f32),
            pltpu.VMEM((N, pad, NMODE), f32),
            DMA((3,)),
            DMA((2, 2, H)),
            DMA((2, 2, H)),
            DMA((2, 2, H)),
            DMA((2, 2, H)),
            DMA,
            DMA,
            DMA((10,)),
            pltpu.VMEM((2, 8, NR), f32),
            pltpu.VMEM((2, CX, NR), f32),
            pltpu.VMEM((2, 8, NR), f32),
            pltpu.VMEM((2, 2, V, NR), f32),
            DMA((2, 2)),
            DMA((2, 2)),
        ],
        compiler_params=pltpu.CompilerParams(
            collective_id=0, has_side_effects=True, vmem_limit_bytes=16 * 2**20
        ),
        name="wake",
    )(
        *(pltpu.with_memory_space_constraint(a, pltpu.HBM) for a in (state.reshape(H * F, rows, NR),
        source.reshape(H * F, rows, NR),
        sigma.reshape(rows, NR),
        *small)),
    )
    fields, amplitudes = store(fields, amplitudes)
    return fields.reshape(state.shape), amplitudes


def solution(mesh):
    field = P(None, None, None, "theta", "xr", None)
    placed = (field, field, P("theta", "xr", None), P("theta")) + (P(),) * 9
    return jax.shard_map(
        functools.partial(local, mesh.shape["theta"], mesh.shape["xr"]),
        mesh=mesh,
        in_specs=placed,
        out_specs=(field, P()),
        check_vma=False,
    )
```
